512 devices in a mesh: gx: 32 (over z_hi, y, x), gz: 16 (over z_lo, core).
Axes of the slice: x: 4, y: 4, z: 16 (z_hi: 2, z_lo: 8; z = z_hi * 8 + z_lo), core: 2. Of those that a mesh axis runs over, the one named last changes fastest.
Arguments:
- field: bfloat16 [2048, 16, 2048], P('gx', None, 'gz'), may hold values from -6 to 6
- even_vectors: bfloat16 [1024, 1024], P('gx', 'gz'), may hold values from -0.1875 to 0.1875
- odd_vectors: bfloat16 [1024, 1024], P('gx', 'gz'), may hold values from -0.1875 to 0.1875
Outputs:
- even_modes: float32 [1024, 16, 2048], P('gx', None, 'gz')
- odd_modes: float32 [1024, 16, 2048], P('gx', None, 'gz')
The draws below stay inside these ranges and needn't reach their ends.
All inputs are finite; a program needn't handle non-finite values.
Results may differ from the reference program's by a relative error of at most 0.0031.
Values may be sent and summed in bfloat16 or wider, within the bound.
A program may use at most 64 MiB of HBM per device.

```python
import jax
import jax.numpy as jnp

WY = 16
NX = 2048
HALF = 1024
NZ = 2048


def shard_levels(key, dims, cuts, smallest, largest):
    level = 1.0
    for axis_at, parts in cuts:
        heights = jax.random.uniform(jax.random.fold_in(jax.random.fold_in(key, 6), axis_at), (parts,), jnp.float32, smallest / len(cuts), largest / len(cuts))
        level = level * jnp.repeat(jnp.exp(heights), dims[axis_at] // parts).reshape((-1,) + (1,) * (len(dims) - 1 - axis_at))
    return level


def bell_draw(rng, extent, scale, bound, pieces=(), held_as=jnp.bfloat16):
    gain = shard_levels(rng, extent, pieces, -0.22, 0.18) if pieces else 1.0
    values = jax.random.normal(rng, extent, jnp.float32) * scale * gain
    return jnp.minimum(jnp.maximum(values, -bound), bound).astype(held_as)


def setup_inputs(seed: int = 0) -> dict:
    keys = jax.random.split(jax.random.key(seed), 4)
    field = bell_draw(keys[0], (NX, WY, NZ), 1.0, 6.0, ((0, 32), (2, 16)))
    even_vectors = bell_draw(keys[1], (HALF, HALF), HALF ** -0.5, 0.1875, ((0, 32), (1, 16)))
    odd_vectors = bell_draw(keys[2], (HALF, HALF), HALF ** -0.5, 0.1875, ((0, 32), (1, 16)))
    return {"field": field, "even_vectors": even_vectors, "odd_vectors": odd_vectors}


def reference(field, even_vectors, odd_vectors):
    flat = field.reshape(NX, WY * NZ)
    lower = flat[:HALF].astype(jnp.float32)
    upper = flat[HALF:][::-1].astype(jnp.float32)
    even_part = (lower + upper).astype(jnp.bfloat16)
    odd_part = (lower - upper).astype(jnp.bfloat16)
    even_modes = jnp.dot(even_vectors, even_part, preferred_element_type=jnp.float32)
    odd_modes = jnp.dot(odd_vectors, odd_part, preferred_element_type=jnp.float32)
    return even_modes.reshape(HALF, WY, NZ), odd_modes.reshape(HALF, WY, NZ)
```

```python
import jax
import jax.numpy as jnp
from jax import lax
from jax.experimental import pallas as pl
from jax.experimental.pallas import tpu as pltpu
from jax.sharding import PartitionSpec as P

MESH = pl.DeviceIdType.MESH
SIDE = 4
PLANE = 16
DEEP = 8
GROUP = 4
ROWS = 64
COLS = 128
MODES = 32
CHUNKS = 8
PER = PLANE // CHUNKS
HOPS = 8


def remote(src, dst, send, recv, target):
    return pltpu.make_async_remote_copy(
        src_ref=src, dst_ref=dst, send_sem=send, recv_sem=recv,
        device_id=target, device_id_type=MESH,
    )


def drain(ref, sem):
    pltpu.make_async_copy(ref, ref, sem).wait()


def kernel(field, even, odd, out_even, out_odd,
           wide, mine, own, far, relay, vecs, acc, sent, got,
           ring_recv, far_recv, recv, send):
    gx, gz = lax.axis_index("gx"), lax.axis_index("gz")
    half = gx // PLANE
    q = lax.rem(gx, PLANE)
    qy, qx = q // SIDE, lax.rem(q, SIDE)
    depth, core = gz // 2, lax.rem(gz, 2)
    z = half * DEEP + depth
    step = 1 - 2 * core

    def at(place, level):
        return ((level // DEEP) * PLANE + place, lax.rem(level, DEEP) * 2 + core)

    def level(k):
        return lax.rem(z + k * step + 2 * DEEP, 2 * DEEP)

    def place(t):
        return lax.rem(qy + t // SIDE, SIDE) * SIDE + lax.rem(qx + lax.rem(t, SIDE), SIDE)

    group = depth // GROUP
    ahead, behind = level(1), level(-1)
    across = half * DEEP + lax.rem(depth + GROUP, DEEP)
    mates = [half * DEEP + group * GROUP + lax.rem(depth + k, GROUP) for k in range(1, GROUP)]
    twin = (gx, gz + step)
    myrows = pl.ds(pl.multiple_of(q * MODES, MODES), MODES)

    barrier = pltpu.get_barrier_semaphore()

    def hello(target):
        pl.semaphore_signal(barrier, inc=1, device_id=target, device_id_type=MESH)

    for t in range(1, PLANE):
        hello(at(place(t), z))
    for t in range(PLANE):
        hello(at(place(t), behind))
    for m in mates:
        hello(at(q, m))
    hello(at(q, across))
    hello(twin)

    wide[...] = field[...].astype(jnp.float32)
    for p in range(PLANE):
        t = lax.rem(p // SIDE - qy + SIDE, SIDE) * SIDE + lax.rem(p % SIDE - qx + SIDE, SIDE)
        mine[t] = wide[pl.ds(p, ROWS, stride=PLANE), :].astype(jnp.bfloat16)
    own[q] = wide[pl.ds(q, ROWS, stride=PLANE), :].astype(jnp.bfloat16)
    vecs[depth, core, myrows, :] = jnp.concatenate([even[...], odd[...]], axis=1)

    pl.semaphore_wait(barrier, 2 * PLANE - 1 + GROUP + 1)

    for c in range(CHUNKS):
        remote(mine.at[pl.ds(c * PER, PER)], relay.at[c], send.at[0], ring_recv.at[c], at(q, ahead)).start()
    for m in mates:
        block = vecs.at[depth, core, myrows]
        remote(block, block, send.at[1], recv.at[0], at(q, m)).start()
    for t in range(1, PLANE):
        remote(mine.at[t], own.at[q], send.at[2], recv.at[1], at(place(t), z)).start()

    def spread(g, k):
        block = vecs.at[pl.ds(g * GROUP, GROUP), core, myrows]
        for t in range(1, PLANE):
            remote(block, block, send.at[3 + k], recv.at[2 + k], at(place(t), z)).start()

    def share(g, k):
        drain(vecs.at[pl.ds(0, GROUP), 0, pl.ds(0, (PLANE - 1) * MODES)], recv.at[2 + k])
        block = vecs.at[pl.ds(g * GROUP, GROUP), core]
        remote(block, block, send.at[5 + k], recv.at[4 + k], twin).start()

    def hop(first, last):
        @pl.loop(first * CHUNKS, last * CHUNKS)
        def _(i):
            drain(relay.at[i], ring_recv.at[i])
            remote(relay.at[i], relay.at[i + CHUNKS], send.at[7], ring_recv.at[i + CHUNKS], at(q, ahead)).start()

    drain(vecs.at[pl.ds(0, GROUP - 1), 0, pl.ds(0, MODES)], recv.at[0])
    block = vecs.at[pl.ds(group * GROUP, GROUP), core, myrows]
    remote(block, block, send.at[8], recv.at[6], at(q, across)).start()
    spread(group, 0)
    hop(0, 2)
    drain(vecs.at[pl.ds(0, GROUP), 0, pl.ds(0, MODES)], recv.at[6])
    spread(1 - group, 1)
    hop(2, 4)
    share(group, 0)
    hop(4, 6)
    share(1 - group, 1)

    @pl.loop(0, CHUNKS)
    def _(c):
        i = (HOPS - 2) * CHUNKS + c
        drain(relay.at[i], ring_recv.at[i])
        for h in range(PER):
            remote(relay.at[i, h], far.at[q], send.at[9], far_recv.at[qy], at(place(c * PER + h), ahead)).start()

    drain(own.at[pl.ds(0, PLANE - 1)], recv.at[1])
    drain(vecs.at[pl.ds(0, GROUP), 0], recv.at[4])
    drain(vecs.at[pl.ds(0, GROUP), 0], recv.at[5])
    wide_rows = SIDE * ROWS
    r = lax.broadcasted_iota(jnp.int32, (wide_rows, wide_rows), 0)
    s = lax.broadcasted_iota(jnp.int32, (wide_rows, wide_rows), 1)
    plain = (r == s).astype(jnp.float32).astype(jnp.bfloat16)
    turned = (r + s == wide_rows - 1).astype(jnp.float32).astype(jnp.bfloat16)
    zero = jnp.zeros((ROWS, COLS), jnp.bfloat16)

    def pick(first):
        return jnp.where(first, plain, turned)

    is_low = jnp.full((wide_rows, wide_rows), half, jnp.int32) == 0
    for_own = jnp.where(is_low, plain, turned)
    for_far = jnp.where(is_low, turned, plain)
    sign = (1 - 2 * half).astype(jnp.float32)
    for ty in range(SIDE):
        g = lax.rem(qy - ty + SIDE, SIDE)
        drain(far.at[pl.ds(0, SIDE)], far_recv.at[g])
        a = own[pl.ds((SIDE - 1 - g) * SIDE, SIDE)].reshape(wide_rows, COLS)
        b = far[pl.ds(g * SIDE, SIDE)].reshape(wide_rows, COLS)
        a = jnp.dot(for_own, a, preferred_element_type=jnp.float32)
        b = jnp.dot(for_far, b, preferred_element_type=jnp.float32)
        plus = (a + b).astype(jnp.bfloat16)
        minus = ((a - b) * sign).astype(jnp.bfloat16)
        j = jnp.where(half == 0, SIDE - 1 - g, g)
        left, right = [], []
        for k in range(2):
            for c in range(2):
                left.append(vecs[2 * j + k, c])
                rows = slice((2 * k + c) * ROWS, (2 * k + c + 1) * ROWS)
                right.append(jnp.concatenate([plus[rows], zero], axis=1))
                right.append(jnp.concatenate([zero, minus[rows]], axis=1))
        part = jnp.dot(jnp.concatenate(left, axis=1), jnp.concatenate(right, axis=0), preferred_element_type=jnp.float32)
        if ty == 0:
            acc[...] = part
        elif ty < SIDE - 1:
            acc[...] += part
        else:
            sent[...] = (acc[...] + part).astype(jnp.bfloat16).reshape(PLANE, MODES, 2 * COLS)

    for t in range(1, PLANE):
        remote(sent.at[place(t)], got.at[q], send.at[10], recv.at[7], at(place(t), z)).start()
    got[q] = sent[q]
    drain(got.at[pl.ds(0, PLANE - 1)], recv.at[7])
    for p in range(PLANE):
        block = got[p].astype(jnp.float32)
        out_even[pl.ds(p, MODES, stride=PLANE), :] = block[:, :COLS]
        out_odd[pl.ds(p, MODES, stride=PLANE), :] = block[:, COLS:]

    drain(mine, send.at[0])
    drain(vecs.at[pl.ds(0, GROUP - 1), 0, pl.ds(0, MODES)], send.at[1])
    drain(mine.at[pl.ds(0, PLANE - 1)], send.at[2])
    for k in range(2):
        drain(vecs.at[pl.ds(0, GROUP), 0, pl.ds(0, (PLANE - 1) * MODES)], send.at[3 + k])
        drain(vecs.at[pl.ds(0, GROUP), 0], send.at[5 + k])
    drain(relay.at[pl.ds(0, (HOPS - 2) * CHUNKS)], send.at[7])
    drain(vecs.at[pl.ds(0, GROUP), 0, pl.ds(0, MODES)], send.at[8])
    drain(mine, send.at[9])
    drain(got.at[pl.ds(0, PLANE - 1)], send.at[10])


def local(field, even_vectors, odd_vectors):
    out = jax.ShapeDtypeStruct((MODES * PLANE, COLS), jnp.float32)
    vmem = pl.BlockSpec(memory_space=pltpu.VMEM)
    slots = (HOPS - 1) * CHUNKS
    even_modes, odd_modes = pl.pallas_call(
        kernel,
        out_shape=(out, out),
        in_specs=[vmem] * 3,
        out_specs=(vmem, vmem),
        scratch_shapes=[
            pltpu.VMEM((ROWS * PLANE, COLS), jnp.float32),
            pltpu.VMEM((PLANE, ROWS, COLS), jnp.bfloat16),
            pltpu.VMEM((PLANE, ROWS, COLS), jnp.bfloat16),
            pltpu.VMEM((PLANE, ROWS, COLS), jnp.bfloat16),
            pltpu.VMEM((slots, PER, ROWS, COLS), jnp.bfloat16),
            pltpu.VMEM((DEEP, 2, PLANE * MODES, COLS), jnp.bfloat16),
            pltpu.VMEM((PLANE * MODES, 2 * COLS), jnp.float32),
            pltpu.VMEM((PLANE, MODES, 2 * COLS), jnp.bfloat16),
            pltpu.VMEM((PLANE, MODES, 2 * COLS), jnp.bfloat16),
            pltpu.SemaphoreType.DMA((slots,)),
            pltpu.SemaphoreType.DMA((SIDE,)),
            pltpu.SemaphoreType.DMA((8,)),
            pltpu.SemaphoreType.DMA((11,)),
        ],
        compiler_params=pltpu.CompilerParams(collective_id=0, has_side_effects=True),
    )(field.reshape(ROWS * PLANE, COLS), even_vectors, odd_vectors)
    return even_modes.reshape(MODES, PLANE, COLS), odd_modes.reshape(MODES, PLANE, COLS)


def solution(mesh):
    return jax.shard_map(
        local,
        mesh=mesh,
        in_specs=(P("gx", None, "gz"), P("gx", "gz"), P("gx", "gz")),
        out_specs=(P("gx", None, "gz"), P("gx", None, "gz")),
        check_vma=False,
    )
```

```python
import jax
import jax.numpy as jnp
from jax import lax
from jax.experimental import pallas as pl
from jax.experimental.pallas import tpu as pltpu
from jax.sharding import PartitionSpec as P

MESH = pl.DeviceIdType.MESH
SIDE = 4
PLANE = 16
DEEP = 8
GROUP = 4
ROWS = 64
COLS = 128
MODES = 32
CHUNKS = 8
PER = PLANE // CHUNKS
HOPS = 8
FAR_FIRST = (2, 3, 1, 0)


def remote(src, dst, send, recv, target):
    return pltpu.make_async_remote_copy(
        src_ref=src, dst_ref=dst, send_sem=send, recv_sem=recv,
        device_id=target, device_id_type=MESH,
    )


def drain(ref, sem):
    pltpu.make_async_copy(ref, ref, sem).wait()


def kernel(field, even, odd, out,
           raw, wide, mine, own, far, relay, vecs, acc, sent, got,
           ring_recv, far_recv, recv, send):
    fetch = pltpu.make_async_copy(field, raw, send.at[11])
    fetch.start()
    gx, gz = lax.axis_index("gx"), lax.axis_index("gz")
    half = gx // PLANE
    q = lax.rem(gx, PLANE)
    qy, qx = q // SIDE, lax.rem(q, SIDE)
    depth, core = gz // 2, lax.rem(gz, 2)
    z = half * DEEP + depth
    step = 1 - 2 * core

    def at(place, level):
        return ((level // DEEP) * PLANE + place, lax.rem(level, DEEP) * 2 + core)

    def level(k):
        return lax.rem(z + k * step + 2 * DEEP, 2 * DEEP)

    def offset(i):
        if isinstance(i, int):
            return FAR_FIRST[i]
        return (1 - i // 2) * (2 + i) + (i // 2) * (3 - i)

    def place(t):
        return lax.rem(qy + offset(t // SIDE), SIDE) * SIDE + lax.rem(qx + offset(t % SIDE if isinstance(t, int) else lax.rem(t, SIDE)), SIDE)

    group = depth // GROUP
    ahead, behind = level(1), level(-1)
    across = half * DEEP + lax.rem(depth + GROUP, DEEP)
    mates = [half * DEEP + group * GROUP + lax.rem(depth + k, GROUP) for k in range(1, GROUP)]
    twin = (gx, gz + step)
    myrows = pl.ds(pl.multiple_of(q * MODES, MODES), MODES)

    barrier = pltpu.get_barrier_semaphore()

    def hello(target):
        pl.semaphore_signal(barrier, inc=1, device_id=target, device_id_type=MESH)

    for t in range(PLANE - 1):
        hello(at(place(t), z))
    for t in range(PLANE):
        hello(at(place(t), behind))
    for m in mates:
        hello(at(q, m))
    hello(at(q, across))
    hello(twin)

    fetch.wait()
    wide[...] = raw[...].astype(jnp.float32)
    for t in range(PLANE):
        mine[t] = wide[pl.ds(place(t), ROWS, stride=PLANE), :].astype(jnp.bfloat16)
    own[q] = mine[PLANE - 1]
    vecs[depth, core, myrows, :] = jnp.concatenate([even[...], odd[...]], axis=1)

    pl.semaphore_wait(barrier, 2 * PLANE - 1 + GROUP + 1)

    for m in mates:
        block = vecs.at[depth, core, myrows]
        remote(block, block, send.at[1], recv.at[0], at(q, m)).start()
    for c in range(CHUNKS):
        remote(mine.at[pl.ds(c * PER, PER)], relay.at[c], send.at[0], ring_recv.at[c], at(q, ahead)).start()
    for t in range(PLANE - 1):
        remote(mine.at[t], own.at[q], send.at[2], recv.at[1], at(place(t), z)).start()

    def spread(g, k):
        block = vecs.at[pl.ds(g * GROUP, GROUP), core, myrows]
        for t in range(PLANE - 1):
            remote(block, block, send.at[3 + k], recv.at[2 + k], at(place(t), z)).start()

    def share(g, k):
        drain(vecs.at[pl.ds(0, GROUP), 0, pl.ds(0, (PLANE - 1) * MODES)], recv.at[2 + k])
        block = vecs.at[pl.ds(g * GROUP, GROUP), core]
        remote(block, block, send.at[5 + k], recv.at[4 + k], twin).start()

    def hop(first, last):
        @pl.loop(first * CHUNKS, last * CHUNKS)
        def _(i):
            drain(relay.at[i], ring_recv.at[i])
            remote(relay.at[i], relay.at[i + CHUNKS], send.at[7], ring_recv.at[i + CHUNKS], at(q, ahead)).start()

    hop(0, 1)
    drain(vecs.at[pl.ds(0, GROUP - 1), 0, pl.ds(0, MODES)], recv.at[0])
    block = vecs.at[pl.ds(group * GROUP, GROUP), core, myrows]
    remote(block, block, send.at[8], recv.at[6], at(q, across)).start()
    spread(group, 0)
    hop(1, 3)
    drain(vecs.at[pl.ds(0, GROUP), 0, pl.ds(0, MODES)], recv.at[6])
    spread(1 - group, 1)
    hop(3, 5)
    share(group, 0)
    hop(5, 6)
    share(1 - group, 1)

    @pl.loop(0, CHUNKS)
    def _(c):
        i = (HOPS - 2) * CHUNKS + c
        drain(relay.at[i], ring_recv.at[i])
        for h in range(PER):
            remote(relay.at[i, h], far.at[q], send.at[9], far_recv.at[qy], at(place(c * PER + h), ahead)).start()

    drain(own.at[pl.ds(0, PLANE - 1)], recv.at[1])
    drain(vecs.at[pl.ds(0, GROUP), 0], recv.at[4])
    drain(vecs.at[pl.ds(0, GROUP), 0], recv.at[5])
    wide_rows = SIDE * ROWS
    r = lax.broadcasted_iota(jnp.int32, (wide_rows, wide_rows), 0)
    s = lax.broadcasted_iota(jnp.int32, (wide_rows, wide_rows), 1)
    plain = (r == s).astype(jnp.float32).astype(jnp.bfloat16)
    turned = (r + s == wide_rows - 1).astype(jnp.float32).astype(jnp.bfloat16)
    zero = jnp.zeros((ROWS, COLS), jnp.bfloat16)

    def pick(first):
        return jnp.where(first, plain, turned)

    is_low = jnp.full((wide_rows, wide_rows), half, jnp.int32) == 0
    for_own = jnp.where(is_low, plain, turned)
    for_far = jnp.where(is_low, turned, plain)
    sign = (1 - 2 * half).astype(jnp.float32)
    for ty in range(SIDE):
        g = lax.rem(qy - offset(ty) + SIDE, SIDE)
        drain(far.at[pl.ds(0, SIDE)], far_recv.at[g])
        a = own[pl.ds((SIDE - 1 - g) * SIDE, SIDE)].reshape(wide_rows, COLS)
        b = far[pl.ds(g * SIDE, SIDE)].reshape(wide_rows, COLS)
        a = jnp.dot(for_own, a, preferred_element_type=jnp.float32)
        b = jnp.dot(for_far, b, preferred_element_type=jnp.float32)
        plus = (a + b).astype(jnp.bfloat16)
        minus = ((a - b) * sign).astype(jnp.bfloat16)
        j = jnp.where(half == 0, SIDE - 1 - g, g)
        left, right = [], []
        for k in range(2):
            for c in range(2):
                left.append(vecs[2 * j + k, c])
                rows = slice((2 * k + c) * ROWS, (2 * k + c + 1) * ROWS)
                right.append(jnp.concatenate([plus[rows], zero], axis=1))
                right.append(jnp.concatenate([zero, minus[rows]], axis=1))
        part = jnp.dot(jnp.concatenate(left, axis=1), jnp.concatenate(right, axis=0), preferred_element_type=jnp.float32)
        if ty == 0:
            acc[...] = part
        elif ty < SIDE - 1:
            acc[...] += part
        else:
            sent[...] = (acc[...] + part).astype(jnp.bfloat16).reshape(PLANE, MODES, 2 * COLS)

    for t in range(PLANE - 1):
        remote(sent.at[place(t)], got.at[q], send.at[10], recv.at[7], at(place(t), z)).start()
    got[q] = sent[q]
    drain(got.at[pl.ds(0, PLANE - 1)], recv.at[7])
    out[...] = got[...]

    drain(mine, send.at[0])
    drain(vecs.at[pl.ds(0, GROUP - 1), 0, pl.ds(0, MODES)], send.at[1])
    drain(mine.at[pl.ds(0, PLANE - 1)], send.at[2])
    for k in range(2):
        drain(vecs.at[pl.ds(0, GROUP), 0, pl.ds(0, (PLANE - 1) * MODES)], send.at[3 + k])
        drain(vecs.at[pl.ds(0, GROUP), 0], send.at[5 + k])
    drain(relay.at[pl.ds(0, (HOPS - 2) * CHUNKS)], send.at[7])
    drain(vecs.at[pl.ds(0, GROUP), 0, pl.ds(0, MODES)], send.at[8])
    drain(mine, send.at[9])
    drain(got.at[pl.ds(0, PLANE - 1)], send.at[10])


def unpack(got, out_even, out_odd):
    rows = got.shape[1]
    for p in range(PLANE):
        block = got[p].astype(jnp.float32)
        out_even[pl.ds(p, rows, stride=PLANE), :] = block[:, :COLS]
        out_odd[pl.ds(p, rows, stride=PLANE), :] = block[:, COLS:]


def local(field, even_vectors, odd_vectors):
    vmem = pl.BlockSpec(memory_space=pltpu.VMEM)
    slots = (HOPS - 1) * CHUNKS
    modes = pl.pallas_call(
        kernel,
        out_shape=jax.ShapeDtypeStruct((PLANE, MODES, 2 * COLS), jnp.bfloat16),
        in_specs=[pl.BlockSpec(memory_space=pl.ANY), vmem, vmem],
        out_specs=vmem,
        scratch_shapes=[
            pltpu.VMEM((ROWS * PLANE, COLS), jnp.bfloat16),
            pltpu.VMEM((ROWS * PLANE, COLS), jnp.float32),
            pltpu.VMEM((PLANE, ROWS, COLS), jnp.bfloat16),
            pltpu.VMEM((PLANE, ROWS, COLS), jnp.bfloat16),
            pltpu.VMEM((PLANE, ROWS, COLS), jnp.bfloat16),
            pltpu.VMEM((slots, PER, ROWS, COLS), jnp.bfloat16),
            pltpu.VMEM((DEEP, 2, PLANE * MODES, COLS), jnp.bfloat16),
            pltpu.VMEM((PLANE * MODES, 2 * COLS), jnp.float32),
            pltpu.VMEM((PLANE, MODES, 2 * COLS), jnp.bfloat16),
            pltpu.VMEM((PLANE, MODES, 2 * COLS), jnp.bfloat16),
            pltpu.SemaphoreType.DMA((slots,)),
            pltpu.SemaphoreType.DMA((SIDE,)),
            pltpu.SemaphoreType.DMA((8,)),
            pltpu.SemaphoreType.DMA((12,)),
        ],
        compiler_params=pltpu.CompilerParams(collective_id=0, has_side_effects=True),
    )(field.reshape(ROWS * PLANE, COLS), even_vectors, odd_vectors)
    parts = 2
    rows = MODES // parts
    out = jax.ShapeDtypeStruct((MODES * PLANE, COLS), jnp.float32)
    even_modes, odd_modes = pl.pallas_call(
        unpack,
        grid=(parts,),
        out_shape=(out, out),
        in_specs=[pl.BlockSpec((PLANE, rows, 2 * COLS), lambda i: (0, i, 0))],
        out_specs=[pl.BlockSpec((rows * PLANE, COLS), lambda i: (i, 0))] * 2,
    )(modes)
    return even_modes.reshape(MODES, PLANE, COLS), odd_modes.reshape(MODES, PLANE, COLS)


def solution(mesh):
    return jax.shard_map(
        local,
        mesh=mesh,
        in_specs=(P("gx", None, "gz"), P("gx", "gz"), P("gx", "gz")),
        out_specs=(P("gx", None, "gz"), P("gx", None, "gz")),
        check_vma=False,
    )
```

```python
import jax
import jax.numpy as jnp
from jax import lax
from jax.experimental import pallas as pl
from jax.experimental.pallas import tpu as pltpu
from jax.sharding import PartitionSpec as P

MESH = pl.DeviceIdType.MESH
SIDE = 4
PLANE = 16
DEEP = 8
GROUP = 4
ROWS = 64
COLS = 128
MODES = 32
CHUNKS = 8
PER = PLANE // CHUNKS
HOPS = 8
FAR_FIRST = (2, 3, 1, 0)


def remote(src, dst, send, recv, target):
    return pltpu.make_async_remote_copy(
        src_ref=src, dst_ref=dst, send_sem=send, recv_sem=recv,
        device_id=target, device_id_type=MESH,
    )


def drain(ref, sem):
    pltpu.make_async_copy(ref, ref, sem).wait()


def kernel(field, even_hbm, odd_hbm, out,
           raw, even, odd, wide, mine, own, far, relay, vecs, acc, sent, got,
           ring_recv, far_recv, recv, send, ready):
    fetches = [
        pltpu.make_async_copy(field, raw, send.at[9]),
        pltpu.make_async_copy(even_hbm, even, send.at[11]),
        pltpu.make_async_copy(odd_hbm, odd, send.at[12]),
    ]
    for fetch in fetches:
        fetch.start()
    gx, gz = lax.axis_index("gx"), lax.axis_index("gz")
    half = gx // PLANE
    q = lax.rem(gx, PLANE)
    qy, qx = q // SIDE, lax.rem(q, SIDE)
    depth, core = gz // 2, lax.rem(gz, 2)
    z = half * DEEP + depth
    step = 2 * core - 1

    def at(place, level):
        return ((level // DEEP) * PLANE + place, lax.rem(level, DEEP) * 2 + core)

    def level(k):
        return lax.rem(z + k * step + 2 * DEEP, 2 * DEEP)

    def offset(i):
        if isinstance(i, int):
            return FAR_FIRST[i]
        return (1 - i // 2) * (2 + i) + (i // 2) * (3 - i)

    def place(t):
        return lax.rem(qy + offset(t // SIDE), SIDE) * SIDE + lax.rem(qx + offset(t % SIDE if isinstance(t, int) else lax.rem(t, SIDE)), SIDE)

    group = depth // GROUP
    ahead, behind = level(1), level(-1)
    across = half * DEEP + lax.rem(depth + GROUP, DEEP)
    mates = [half * DEEP + group * GROUP + lax.rem(depth + k, GROUP) for k in range(1, GROUP)]
    twin = (gx, gz + 1 - 2 * core)
    myrows = pl.ds(pl.multiple_of(q * MODES, MODES), MODES)

    barrier = pltpu.get_barrier_semaphore()

    def hello(target):
        pl.semaphore_signal(barrier, inc=1, device_id=target, device_id_type=MESH)

    for t in range(PLANE - 1):
        hello(at(place(t), z))
    hello(at(q, ahead))
    hello(at(q, behind))
    for m in mates:
        hello(at(q, m))
    hello(at(q, across))
    hello(twin)

    for fetch in fetches:
        fetch.wait()
    wide[...] = raw[...].astype(jnp.float32)
    for t in range(PLANE):
        mine[t] = wide[pl.ds(place(t), ROWS, stride=PLANE), :].astype(jnp.bfloat16)
    own[q] = mine[PLANE - 1]
    vecs[depth, core, myrows, :] = jnp.concatenate([even[...], odd[...]], axis=1)

    pl.semaphore_wait(barrier, PLANE - 1 + 2 + GROUP + 1)

    for m in mates:
        block = vecs.at[depth, core, myrows]
        remote(block, block, send.at[1], recv.at[0], at(q, m)).start()
    for c in range(CHUNKS):
        remote(mine.at[pl.ds(c * PER, PER)], relay.at[c], send.at[0], ring_recv.at[c], at(q, ahead)).start()
    pl.semaphore_signal(ready, inc=1, device_id=at(q, behind), device_id_type=MESH)
    for t in range(PLANE - 1):
        remote(mine.at[t], own.at[q], send.at[2], recv.at[1], at(place(t), z)).start()

    def spread(g, k):
        block = vecs.at[pl.ds(g * GROUP, GROUP), core, myrows]
        for t in range(PLANE - 1):
            remote(block, block, send.at[3 + k], recv.at[2 + k], at(place(t), z)).start()

    def share(g, k):
        drain(vecs.at[pl.ds(0, GROUP), 0, pl.ds(0, (PLANE - 1) * MODES)], recv.at[2 + k])
        block = vecs.at[pl.ds(g * GROUP, GROUP), core]
        remote(block, block, send.at[5 + k], recv.at[4 + k], twin).start()

    def hop(first, last):
        @pl.loop(first * CHUNKS, last * CHUNKS)
        def _(i):
            drain(relay.at[i], ring_recv.at[i])
            remote(relay.at[i], relay.at[i + CHUNKS], send.at[7], ring_recv.at[i + CHUNKS], at(q, ahead)).start()

    hop(0, 1)
    drain(vecs.at[pl.ds(0, GROUP - 1), 0, pl.ds(0, MODES)], recv.at[0])
    block = vecs.at[pl.ds(group * GROUP, GROUP), core, myrows]
    remote(block, block, send.at[8], recv.at[6], at(q, across)).start()
    spread(group, 0)
    hop(1, 3)
    drain(vecs.at[pl.ds(0, GROUP), 0, pl.ds(0, MODES)], recv.at[6])
    spread(1 - group, 1)
    hop(3, 5)
    share(group, 0)
    hop(5, 6)
    share(1 - group, 1)

    pl.semaphore_wait(ready, 1)

    @pl.loop(0, CHUNKS)
    def _(c):
        i = (HOPS - 2) * CHUNKS + c
        drain(relay.at[i], ring_recv.at[i])
        for h in range(PER):
            remote(relay.at[i, h], far.at[q], send.at[13], far_recv.at[qy], at(place(c * PER + h), ahead)).start()

    drain(own.at[pl.ds(0, PLANE - 1)], recv.at[1])
    drain(vecs.at[pl.ds(0, GROUP), 0], recv.at[4])
    drain(vecs.at[pl.ds(0, GROUP), 0], recv.at[5])
    wide_rows = SIDE * ROWS
    r = lax.broadcasted_iota(jnp.int32, (wide_rows, wide_rows), 0)
    s = lax.broadcasted_iota(jnp.int32, (wide_rows, wide_rows), 1)
    plain = (r == s).astype(jnp.float32).astype(jnp.bfloat16)
    turned = (r + s == wide_rows - 1).astype(jnp.float32).astype(jnp.bfloat16)
    zero = jnp.zeros((ROWS, COLS), jnp.bfloat16)

    def pick(first):
        return jnp.where(first, plain, turned)

    is_low = jnp.full((wide_rows, wide_rows), half, jnp.int32) == 0
    for_own = jnp.where(is_low, plain, turned)
    for_far = jnp.where(is_low, turned, plain)
    sign = (1 - 2 * half).astype(jnp.float32)
    for ty in range(SIDE):
        g = lax.rem(qy - offset(ty) + SIDE, SIDE)
        drain(far.at[pl.ds(0, SIDE)], far_recv.at[g])
        a = own[pl.ds((SIDE - 1 - g) * SIDE, SIDE)].reshape(wide_rows, COLS)
        b = far[pl.ds(g * SIDE, SIDE)].reshape(wide_rows, COLS)
        a = jnp.dot(for_own, a, preferred_element_type=jnp.float32)
        b = jnp.dot(for_far, b, preferred_element_type=jnp.float32)
        plus = (a + b).astype(jnp.bfloat16)
        minus = ((a - b) * sign).astype(jnp.bfloat16)
        j = jnp.where(half == 0, SIDE - 1 - g, g)
        left, right = [], []
        for k in range(2):
            for c in range(2):
                left.append(vecs[2 * j + k, c])
                rows = slice((2 * k + c) * ROWS, (2 * k + c + 1) * ROWS)
                right.append(jnp.concatenate([plus[rows], zero], axis=1))
                right.append(jnp.concatenate([zero, minus[rows]], axis=1))
        part = jnp.dot(jnp.concatenate(left, axis=1), jnp.concatenate(right, axis=0), preferred_element_type=jnp.float32)
        if ty == 0:
            acc[...] = part
        elif ty < SIDE - 1:
            acc[...] += part
        else:
            sent[...] = (acc[...] + part).astype(jnp.bfloat16).reshape(PLANE, MODES, 2 * COLS)

    for t in range(PLANE - 1):
        remote(sent.at[place(t)], got.at[q], send.at[10], recv.at[7], at(place(t), z)).start()
    got[q] = sent[q]
    drain(got.at[pl.ds(0, PLANE - 1)], recv.at[7])
    out[...] = got[...]

    drain(mine, send.at[0])
    drain(vecs.at[pl.ds(0, GROUP - 1), 0, pl.ds(0, MODES)], send.at[1])
    drain(mine.at[pl.ds(0, PLANE - 1)], send.at[2])
    for k in range(2):
        drain(vecs.at[pl.ds(0, GROUP), 0, pl.ds(0, (PLANE - 1) * MODES)], send.at[3 + k])
        drain(vecs.at[pl.ds(0, GROUP), 0], send.at[5 + k])
    drain(relay.at[pl.ds(0, (HOPS - 2) * CHUNKS)], send.at[7])
    drain(vecs.at[pl.ds(0, GROUP), 0, pl.ds(0, MODES)], send.at[8])
    drain(mine, send.at[13])
    drain(got.at[pl.ds(0, PLANE - 1)], send.at[10])


def unpack(got, out_even, out_odd):
    rows = got.shape[1]
    for p in range(PLANE):
        block = got[p].astype(jnp.float32)
        out_even[pl.ds(p, rows, stride=PLANE), :] = block[:, :COLS]
        out_odd[pl.ds(p, rows, stride=PLANE), :] = block[:, COLS:]


def local(field, even_vectors, odd_vectors):
    vmem = pl.BlockSpec(memory_space=pltpu.VMEM)
    slots = (HOPS - 1) * CHUNKS
    modes = pl.pallas_call(
        kernel,
        out_shape=jax.ShapeDtypeStruct((PLANE, MODES, 2 * COLS), jnp.bfloat16),
        in_specs=[pl.BlockSpec(memory_space=pltpu.HBM)] * 3,
        out_specs=vmem,
        scratch_shapes=[
            pltpu.VMEM((ROWS * PLANE, COLS), jnp.bfloat16),
            pltpu.VMEM((MODES, ROWS), jnp.bfloat16),
            pltpu.VMEM((MODES, ROWS), jnp.bfloat16),
            pltpu.VMEM((ROWS * PLANE, COLS), jnp.float32),
            pltpu.VMEM((PLANE, ROWS, COLS), jnp.bfloat16),
            pltpu.VMEM((PLANE, ROWS, COLS), jnp.bfloat16),
            pltpu.VMEM((PLANE, ROWS, COLS), jnp.bfloat16),
            pltpu.VMEM((slots, PER, ROWS, COLS), jnp.bfloat16),
            pltpu.VMEM((DEEP, 2, PLANE * MODES, COLS), jnp.bfloat16),
            pltpu.VMEM((PLANE * MODES, 2 * COLS), jnp.float32),
            pltpu.VMEM((PLANE, MODES, 2 * COLS), jnp.bfloat16),
            pltpu.VMEM((PLANE, MODES, 2 * COLS), jnp.bfloat16),
            pltpu.SemaphoreType.DMA((slots,)),
            pltpu.SemaphoreType.DMA((SIDE,)),
            pltpu.SemaphoreType.DMA((8,)),
            pltpu.SemaphoreType.DMA((14,)),
            pltpu.SemaphoreType.REGULAR,
        ],
        compiler_params=pltpu.CompilerParams(collective_id=0, has_side_effects=True, vmem_limit_bytes=16 * 1024 * 1024),
    )(field.reshape(ROWS * PLANE, COLS), even_vectors, odd_vectors)
    parts = 2
    rows = MODES // parts
    out = jax.ShapeDtypeStruct((MODES * PLANE, COLS), jnp.float32)
    even_modes, odd_modes = pl.pallas_call(
        unpack,
        grid=(parts,),
        out_shape=(out, out),
        in_specs=[pl.BlockSpec((PLANE, rows, 2 * COLS), lambda i: (0, i, 0))],
        out_specs=[pl.BlockSpec((rows * PLANE, COLS), lambda i: (i, 0))] * 2,
        compiler_params=pltpu.CompilerParams(vmem_limit_bytes=8 * 1024 * 1024),
    )(modes)
    return even_modes.reshape(MODES, PLANE, COLS), odd_modes.reshape(MODES, PLANE, COLS)


def solution(mesh):
    return jax.shard_map(
        local,
        mesh=mesh,
        in_specs=(P("gx", None, "gz"), P("gx", "gz"), P("gx", "gz")),
        out_specs=(P("gx", None, "gz"), P("gx", None, "gz")),
        check_vma=False,
    )
```

```python
import jax
import jax.numpy as jnp
from jax import lax
from jax.experimental import pallas as pl
from jax.experimental.pallas import tpu as pltpu
from jax.sharding import PartitionSpec as P

MESH = pl.DeviceIdType.MESH
SIDE = 4
PLANE = 16
DEEP = 8
GROUP = 4
ROWS = 64
COLS = 128
MODES = 32
CHUNKS = 8
PER = PLANE // CHUNKS
HOPS = 8
FAR_FIRST = (2, 3, 1, 0)


def remote(src, dst, send, recv, target):
    return pltpu.make_async_remote_copy(
        src_ref=src, dst_ref=dst, send_sem=send, recv_sem=recv,
        device_id=target, device_id_type=MESH,
    )


def drain(ref, sem):
    pltpu.make_async_copy(ref, ref, sem).wait()


def kernel(field, even_hbm, odd_hbm, out,
           raw, even, odd, wide, mine, own, far, relay, vecs, acc, sent, got,
           ring_recv, far_recv, recv, send, ready):
    fetches = [
        pltpu.make_async_copy(field, raw, send.at[9]),
        pltpu.make_async_copy(even_hbm, even, send.at[11]),
        pltpu.make_async_copy(odd_hbm, odd, send.at[12]),
    ]
    for fetch in fetches:
        fetch.start()
    gx, gz = lax.axis_index("gx"), lax.axis_index("gz")
    half = gx // PLANE
    q = lax.rem(gx, PLANE)
    qy, qx = q // SIDE, lax.rem(q, SIDE)
    depth, core = gz // 2, lax.rem(gz, 2)
    z = half * DEEP + depth
    step = 2 * core - 1

    def at(place, level):
        return ((level // DEEP) * PLANE + place, lax.rem(level, DEEP) * 2 + core)

    def level(k):
        return lax.rem(z + k * step + 2 * DEEP, 2 * DEEP)

    def offset(i):
        if isinstance(i, int):
            return FAR_FIRST[i]
        return (1 - i // 2) * (2 + i) + (i // 2) * (3 - i)

    def place(t):
        return lax.rem(qy + offset(t // SIDE), SIDE) * SIDE + lax.rem(qx + offset(t % SIDE if isinstance(t, int) else lax.rem(t, SIDE)), SIDE)

    group = depth // GROUP
    ahead, behind = level(1), level(-1)
    across = half * DEEP + lax.rem(depth + GROUP, DEEP)
    mates = [half * DEEP + group * GROUP + lax.rem(depth + k, GROUP) for k in range(1, GROUP)]
    twin = (gx, gz + 1 - 2 * core)
    myrows = pl.ds(pl.multiple_of(q * MODES, MODES), MODES)

    barrier = pltpu.get_barrier_semaphore()

    def hello(target):
        pl.semaphore_signal(barrier, inc=1, device_id=target, device_id_type=MESH)

    for t in range(PLANE - 1):
        hello(at(place(t), z))
    hello(at(q, ahead))
    hello(at(q, behind))
    for m in mates:
        hello(at(q, m))
    hello(at(q, across))
    hello(twin)

    for fetch in fetches:
        fetch.wait()
    wide[...] = raw[...].astype(jnp.float32)
    for t in range(PLANE):
        mine[t] = wide[pl.ds(place(t), ROWS, stride=PLANE), :].astype(jnp.bfloat16)
    own[q] = mine[PLANE - 1]
    vecs[depth, core, myrows, :] = jnp.concatenate([even[...], odd[...]], axis=1)

    pl.semaphore_wait(barrier, PLANE - 1 + 2 + GROUP + 1)

    for m in mates:
        block = vecs.at[depth, core, myrows]
        remote(block, block, send.at[1], recv.at[0], at(q, m)).start()
    for c in range(CHUNKS):
        remote(mine.at[pl.ds(c * PER, PER)], relay.at[c], send.at[0], ring_recv.at[c], at(q, ahead)).start()
    pl.semaphore_signal(ready, inc=1, device_id=at(q, behind), device_id_type=MESH)
    for t in range(PLANE - 1):
        remote(mine.at[t], own.at[q], send.at[2], recv.at[1], at(place(t), z)).start()

    def spread(g, k):
        block = vecs.at[pl.ds(g * GROUP, GROUP), core, myrows]
        for t in range(PLANE - 1):
            remote(block, block, send.at[3 + k], recv.at[2 + k], at(place(t), z)).start()

    def share(g, k):
        drain(vecs.at[pl.ds(0, GROUP), 0, pl.ds(0, (PLANE - 1) * MODES)], recv.at[2 + k])
        block = vecs.at[pl.ds(g * GROUP, GROUP), core]
        remote(block, block, send.at[5 + k], recv.at[4 + k], twin).start()

    def hop(first, last):
        @pl.loop(first * CHUNKS, last * CHUNKS)
        def _(i):
            drain(relay.at[i], ring_recv.at[i])
            remote(relay.at[i], relay.at[i + CHUNKS], send.at[7], ring_recv.at[i + CHUNKS], at(q, ahead)).start()

    hop(0, 1)
    drain(vecs.at[pl.ds(0, GROUP - 1), 0, pl.ds(0, MODES)], recv.at[0])
    block = vecs.at[pl.ds(group * GROUP, GROUP), core, myrows]
    remote(block, block, send.at[8], recv.at[6], at(q, across)).start()
    spread(group, 0)
    hop(1, 3)
    drain(vecs.at[pl.ds(0, GROUP), 0, pl.ds(0, MODES)], recv.at[6])
    spread(1 - group, 1)
    hop(3, 5)
    share(group, 0)
    hop(5, 6)
    share(1 - group, 1)

    pl.semaphore_wait(ready, 1)

    @pl.loop(0, CHUNKS)
    def _(c):
        i = (HOPS - 2) * CHUNKS + c
        drain(relay.at[i], ring_recv.at[i])
        for h in range(PER):
            remote(relay.at[i, h], far.at[q], send.at[13], far_recv.at[qy], at(place(c * PER + h), ahead)).start()

    drain(own.at[pl.ds(0, PLANE - 1)], recv.at[1])
    drain(vecs.at[pl.ds(0, GROUP), 0], recv.at[4])
    drain(vecs.at[pl.ds(0, GROUP), 0], recv.at[5])
    wide_rows = SIDE * ROWS
    r = lax.broadcasted_iota(jnp.int32, (wide_rows, wide_rows), 0)
    s = lax.broadcasted_iota(jnp.int32, (wide_rows, wide_rows), 1)
    plain = (r == s).astype(jnp.float32).astype(jnp.bfloat16)
    turned = (r + s == wide_rows - 1).astype(jnp.float32).astype(jnp.bfloat16)
    zero = jnp.zeros((ROWS, COLS), jnp.bfloat16)

    def pick(first):
        return jnp.where(first, plain, turned)

    is_low = jnp.full((wide_rows, wide_rows), half, jnp.int32) == 0
    for_own = jnp.where(is_low, plain, turned)
    for_far = jnp.where(is_low, turned, plain)
    sign = (1 - 2 * half).astype(jnp.float32)
    for ty in range(SIDE):
        g = lax.rem(qy - offset(ty) + SIDE, SIDE)
        drain(far.at[pl.ds(0, SIDE)], far_recv.at[g])
        a = own[pl.ds((SIDE - 1 - g) * SIDE, SIDE)].reshape(wide_rows, COLS)
        b = far[pl.ds(g * SIDE, SIDE)].reshape(wide_rows, COLS)
        a = jnp.dot(for_own, a, preferred_element_type=jnp.float32)
        b = jnp.dot(for_far, b, preferred_element_type=jnp.float32)
        plus = (a + b).astype(jnp.bfloat16)
        minus = ((a - b) * sign).astype(jnp.bfloat16)
        j = jnp.where(half == 0, SIDE - 1 - g, g)
        left, right = [], []
        for k in range(2):
            for c in range(2):
                left.append(vecs[2 * j + k, c])
                rows = slice((2 * k + c) * ROWS, (2 * k + c + 1) * ROWS)
                right.append(jnp.concatenate([plus[rows], zero], axis=1))
                right.append(jnp.concatenate([zero, minus[rows]], axis=1))
        part = jnp.dot(jnp.concatenate(left, axis=1), jnp.concatenate(right, axis=0), preferred_element_type=jnp.float32)
        if ty == 0:
            acc[...] = part
        elif ty < SIDE - 1:
            acc[...] += part
        else:
            sent[...] = (acc[...] + part).astype(jnp.bfloat16).reshape(PLANE, MODES, 2 * COLS)

    for t in range(PLANE - 1):
        remote(sent.at[place(t)], got.at[q], send.at[10], recv.at[7], at(place(t), z)).start()
    got[q] = sent[q]
    drain(got.at[pl.ds(0, PLANE - 1)], recv.at[7])
    out[...] = got[...]

    drain(mine, send.at[0])
    drain(vecs.at[pl.ds(0, GROUP - 1), 0, pl.ds(0, MODES)], send.at[1])
    drain(mine.at[pl.ds(0, PLANE - 1)], send.at[2])
    for k in range(2):
        drain(vecs.at[pl.ds(0, GROUP), 0, pl.ds(0, (PLANE - 1) * MODES)], send.at[3 + k])
        drain(vecs.at[pl.ds(0, GROUP), 0], send.at[5 + k])
    drain(relay.at[pl.ds(0, (HOPS - 2) * CHUNKS)], send.at[7])
    drain(vecs.at[pl.ds(0, GROUP), 0, pl.ds(0, MODES)], send.at[8])
    drain(mine, send.at[13])
    drain(got.at[pl.ds(0, PLANE - 1)], send.at[10])


def unpack(got, out_even, out_odd):
    rows = got.shape[1]
    for p in range(PLANE):
        block = got[p].astype(jnp.float32)
        out_even[pl.ds(p, rows, stride=PLANE), :] = block[:, :COLS]
        out_odd[pl.ds(p, rows, stride=PLANE), :] = block[:, COLS:]


def local(field, even_vectors, odd_vectors):
    vmem = pl.BlockSpec(memory_space=pltpu.VMEM)
    slots = (HOPS - 1) * CHUNKS
    modes = pl.pallas_call(
        kernel,
        out_shape=jax.ShapeDtypeStruct((PLANE, MODES, 2 * COLS), jnp.bfloat16),
        in_specs=[pl.BlockSpec(memory_space=pltpu.HBM)] * 3,
        out_specs=vmem,
        scratch_shapes=[
            pltpu.VMEM((ROWS * PLANE, COLS), jnp.bfloat16),
            pltpu.VMEM((MODES, ROWS), jnp.bfloat16),
            pltpu.VMEM((MODES, ROWS), jnp.bfloat16),
            pltpu.VMEM((ROWS * PLANE, COLS), jnp.float32),
            pltpu.VMEM((PLANE, ROWS, COLS), jnp.bfloat16),
            pltpu.VMEM((PLANE, ROWS, COLS), jnp.bfloat16),
            pltpu.VMEM((PLANE, ROWS, COLS), jnp.bfloat16),
            pltpu.VMEM((slots, PER, ROWS, COLS), jnp.bfloat16),
            pltpu.VMEM((DEEP, 2, PLANE * MODES, COLS), jnp.bfloat16),
            pltpu.VMEM((PLANE * MODES, 2 * COLS), jnp.float32),
            pltpu.VMEM((PLANE, MODES, 2 * COLS), jnp.bfloat16),
            pltpu.VMEM((PLANE, MODES, 2 * COLS), jnp.bfloat16),
            pltpu.SemaphoreType.DMA((slots,)),
            pltpu.SemaphoreType.DMA((SIDE,)),
            pltpu.SemaphoreType.DMA((8,)),
            pltpu.SemaphoreType.DMA((14,)),
            pltpu.SemaphoreType.REGULAR,
        ],
        compiler_params=pltpu.CompilerParams(collective_id=0, has_side_effects=True, vmem_limit_bytes=16 * 1024 * 1024),
    )(*(pltpu.with_memory_space_constraint(v, pltpu.HBM) for v in (field.reshape(ROWS * PLANE, COLS), even_vectors, odd_vectors)))
    parts = 2
    rows = MODES // parts
    out = jax.ShapeDtypeStruct((MODES * PLANE, COLS), jnp.float32)
    even_modes, odd_modes = pl.pallas_call(
        unpack,
        grid=(parts,),
        out_shape=(out, out),
        in_specs=[pl.BlockSpec((PLANE, rows, 2 * COLS), lambda i: (0, i, 0))],
        out_specs=[pl.BlockSpec((rows * PLANE, COLS), lambda i: (i, 0))] * 2,
        compiler_params=pltpu.CompilerParams(vmem_limit_bytes=8 * 1024 * 1024),
    )(modes)
    return even_modes.reshape(MODES, PLANE, COLS), odd_modes.reshape(MODES, PLANE, COLS)


def solution(mesh):
    return jax.shard_map(
        local,
        mesh=mesh,
        in_specs=(P("gx", None, "gz"), P("gx", "gz"), P("gx", "gz")),
        out_specs=(P("gx", None, "gz"), P("gx", None, "gz")),
        check_vma=False,
    )
```

```python
import jax
import jax.numpy as jnp
from jax import lax
from jax.experimental import pallas as pl
from jax.experimental.pallas import tpu as pltpu
from jax.sharding import PartitionSpec as P

MESH = pl.DeviceIdType.MESH
SIDE = 4
PLANE = 16
DEEP = 8
GROUP = 4
ROWS = 64
COLS = 128
MODES = 32
CHUNKS = 16
PER = PLANE // CHUNKS
HOPS = 8
FAR_FIRST = (2, 3, 1, 0)


def remote(src, dst, send, recv, target):
    return pltpu.make_async_remote_copy(
        src_ref=src, dst_ref=dst, send_sem=send, recv_sem=recv,
        device_id=target, device_id_type=MESH,
    )


def drain(ref, sem):
    pltpu.make_async_copy(ref, ref, sem).wait()


def kernel(field, even_hbm, odd_hbm, out,
           raw, even, odd, wide, mine, own, far, relay, vecs, acc, sent, got,
           ring_recv, far_recv, recv, send, ready):
    fetches = [
        pltpu.make_async_copy(field, raw, send.at[9]),
        pltpu.make_async_copy(even_hbm, even, send.at[11]),
        pltpu.make_async_copy(odd_hbm, odd, send.at[12]),
    ]
    for fetch in fetches:
        fetch.start()
    gx, gz = lax.axis_index("gx"), lax.axis_index("gz")
    half = gx // PLANE
    q = lax.rem(gx, PLANE)
    qy, qx = q // SIDE, lax.rem(q, SIDE)
    depth, core = gz // 2, lax.rem(gz, 2)
    z = half * DEEP + depth
    step = 2 * core - 1

    def at(place, level):
        return ((level // DEEP) * PLANE + place, lax.rem(level, DEEP) * 2 + core)

    def level(k):
        return lax.rem(z + k * step + 2 * DEEP, 2 * DEEP)

    def offset(i):
        if isinstance(i, int):
            return FAR_FIRST[i]
        return (1 - i // 2) * (2 + i) + (i // 2) * (3 - i)

    def place(t):
        return lax.rem(qy + offset(t // SIDE), SIDE) * SIDE + lax.rem(qx + offset(t % SIDE if isinstance(t, int) else lax.rem(t, SIDE)), SIDE)

    group = depth // GROUP
    ahead, behind = level(1), level(-1)
    across = half * DEEP + lax.rem(depth + GROUP, DEEP)
    mates = [half * DEEP + group * GROUP + lax.rem(depth + k, GROUP) for k in range(1, GROUP)]
    twin = (gx, gz + 1 - 2 * core)
    myrows = pl.ds(pl.multiple_of(q * MODES, MODES), MODES)

    barrier = pltpu.get_barrier_semaphore()

    def hello(target):
        pl.semaphore_signal(barrier, inc=1, device_id=target, device_id_type=MESH)

    hello(at(q, across))
    for m in mates:
        hello(at(q, m))
    hello(at(q, ahead))
    hello(at(q, behind))
    for t in range(PLANE - 1):
        hello(at(place(t), z))
    hello(twin)

    for fetch in fetches:
        fetch.wait()
    wide[...] = raw[...].astype(jnp.float32)
    for t in range(PLANE):
        mine[t] = wide[pl.ds(place(t), ROWS, stride=PLANE), :].astype(jnp.bfloat16)
    own[q] = mine[PLANE - 1]
    vecs[depth, core, myrows, :] = jnp.concatenate([even[...], odd[...]], axis=1)

    pl.semaphore_wait(barrier, PLANE - 1 + 2 + GROUP + 1)

    for m in mates:
        block = vecs.at[depth, core, myrows]
        remote(block, block, send.at[1], recv.at[0], at(q, m)).start()
    for c in range(CHUNKS):
        remote(mine.at[pl.ds(c * PER, PER)], relay.at[c], send.at[0], ring_recv.at[c], at(q, ahead)).start()
    pl.semaphore_signal(ready, inc=1, device_id=at(q, behind), device_id_type=MESH)
    for t in range(PLANE - 1):
        remote(mine.at[t], own.at[q], send.at[2], recv.at[1], at(place(t), z)).start()

    def spread(g, k):
        block = vecs.at[pl.ds(g * GROUP, GROUP), core, myrows]
        for t in range(PLANE - 1):
            remote(block, block, send.at[3 + k], recv.at[2 + k], at(place(t), z)).start()

    def share(g, k):
        drain(vecs.at[pl.ds(0, GROUP), 0, pl.ds(0, (PLANE - 1) * MODES)], recv.at[2 + k])
        block = vecs.at[pl.ds(g * GROUP, GROUP), core]
        remote(block, block, send.at[5 + k], recv.at[4 + k], twin).start()

    def hop(first, last):
        @pl.loop(first * CHUNKS, last * CHUNKS)
        def _(i):
            drain(relay.at[i], ring_recv.at[i])
            remote(relay.at[i], relay.at[i + CHUNKS], send.at[7], ring_recv.at[i + CHUNKS], at(q, ahead)).start()

    hop(0, 1)
    drain(vecs.at[pl.ds(0, GROUP - 1), 0, pl.ds(0, MODES)], recv.at[0])
    block = vecs.at[pl.ds(group * GROUP, GROUP), core, myrows]
    remote(block, block, send.at[8], recv.at[6], at(q, across)).start()
    spread(group, 0)
    hop(1, 3)
    drain(vecs.at[pl.ds(0, GROUP), 0, pl.ds(0, MODES)], recv.at[6])
    spread(1 - group, 1)
    hop(3, 5)
    share(group, 0)
    hop(5, 6)
    share(1 - group, 1)

    pl.semaphore_wait(ready, 1)

    @pl.loop(0, CHUNKS)
    def _(c):
        i = (HOPS - 2) * CHUNKS + c
        drain(relay.at[i], ring_recv.at[i])
        for h in range(PER):
            remote(relay.at[i, h], far.at[q], send.at[13], far_recv.at[qy], at(place(c * PER + h), ahead)).start()

    drain(own.at[pl.ds(0, PLANE - 1)], recv.at[1])
    drain(vecs.at[pl.ds(0, GROUP), 0], recv.at[4])
    drain(vecs.at[pl.ds(0, GROUP), 0], recv.at[5])
    wide_rows = SIDE * ROWS
    r = lax.broadcasted_iota(jnp.int32, (wide_rows, wide_rows), 0)
    s = lax.broadcasted_iota(jnp.int32, (wide_rows, wide_rows), 1)
    plain = (r == s).astype(jnp.float32).astype(jnp.bfloat16)
    turned = (r + s == wide_rows - 1).astype(jnp.float32).astype(jnp.bfloat16)
    zero = jnp.zeros((ROWS, COLS), jnp.bfloat16)

    def pick(first):
        return jnp.where(first, plain, turned)

    is_low = jnp.full((wide_rows, wide_rows), half, jnp.int32) == 0
    for_own = jnp.where(is_low, plain, turned)
    for_far = jnp.where(is_low, turned, plain)
    sign = (1 - 2 * half).astype(jnp.float32)
    for ty in range(SIDE):
        g = lax.rem(qy - offset(ty) + SIDE, SIDE)
        a = own[pl.ds((SIDE - 1 - g) * SIDE, SIDE)].reshape(wide_rows, COLS)
        a = jnp.dot(for_own, a, preferred_element_type=jnp.float32)
        drain(far.at[pl.ds(0, SIDE)], far_recv.at[g])
        b = far[pl.ds(g * SIDE, SIDE)].reshape(wide_rows, COLS)
        b = jnp.dot(for_far, b, preferred_element_type=jnp.float32)
        plus = (a + b).astype(jnp.bfloat16)
        minus = ((a - b) * sign).astype(jnp.bfloat16)
        j = jnp.where(half == 0, SIDE - 1 - g, g)
        left, right = [], []
        for k in range(2):
            for c in range(2):
                left.append(vecs[2 * j + k, c])
                rows = slice((2 * k + c) * ROWS, (2 * k + c + 1) * ROWS)
                right.append(jnp.concatenate([plus[rows], zero], axis=1))
                right.append(jnp.concatenate([zero, minus[rows]], axis=1))
        part = jnp.dot(jnp.concatenate(left, axis=1), jnp.concatenate(right, axis=0), preferred_element_type=jnp.float32)
        if ty == 0:
            acc[...] = part
        elif ty < SIDE - 1:
            acc[...] += part
        else:
            sent[...] = (acc[...] + part).astype(jnp.bfloat16).reshape(PLANE, MODES, 2 * COLS)

    for t in range(PLANE - 1):
        remote(sent.at[place(t)], got.at[q], send.at[10], recv.at[7], at(place(t), z)).start()
    got[q] = sent[q]
    drain(got.at[pl.ds(0, PLANE - 1)], recv.at[7])
    out[...] = got[...]

    drain(mine, send.at[0])
    drain(vecs.at[pl.ds(0, GROUP - 1), 0, pl.ds(0, MODES)], send.at[1])
    drain(mine.at[pl.ds(0, PLANE - 1)], send.at[2])
    for k in range(2):
        drain(vecs.at[pl.ds(0, GROUP), 0, pl.ds(0, (PLANE - 1) * MODES)], send.at[3 + k])
        drain(vecs.at[pl.ds(0, GROUP), 0], send.at[5 + k])
    drain(relay.at[pl.ds(0, (HOPS - 2) * CHUNKS)], send.at[7])
    drain(vecs.at[pl.ds(0, GROUP), 0, pl.ds(0, MODES)], send.at[8])
    drain(mine, send.at[13])
    drain(got.at[pl.ds(0, PLANE - 1)], send.at[10])


def unpack(got, out_even, out_odd):
    rows = got.shape[1]
    for p in range(PLANE):
        block = got[p].astype(jnp.float32)
        out_even[pl.ds(p, rows, stride=PLANE), :] = block[:, :COLS]
        out_odd[pl.ds(p, rows, stride=PLANE), :] = block[:, COLS:]


def local(field, even_vectors, odd_vectors):
    vmem = pl.BlockSpec(memory_space=pltpu.VMEM)
    slots = (HOPS - 1) * CHUNKS
    modes = pl.pallas_call(
        kernel,
        out_shape=jax.ShapeDtypeStruct((PLANE, MODES, 2 * COLS), jnp.bfloat16),
        in_specs=[pl.BlockSpec(memory_space=pltpu.HBM)] * 3,
        out_specs=vmem,
        scratch_shapes=[
            pltpu.VMEM((ROWS * PLANE, COLS), jnp.bfloat16),
            pltpu.VMEM((MODES, ROWS), jnp.bfloat16),
            pltpu.VMEM((MODES, ROWS), jnp.bfloat16),
            pltpu.VMEM((ROWS * PLANE, COLS), jnp.float32),
            pltpu.VMEM((PLANE, ROWS, COLS), jnp.bfloat16),
            pltpu.VMEM((PLANE, ROWS, COLS), jnp.bfloat16),
            pltpu.VMEM((PLANE, ROWS, COLS), jnp.bfloat16),
            pltpu.VMEM((slots, PER, ROWS, COLS), jnp.bfloat16),
            pltpu.VMEM((DEEP, 2, PLANE * MODES, COLS), jnp.bfloat16),
            pltpu.VMEM((PLANE * MODES, 2 * COLS), jnp.float32),
            pltpu.VMEM((PLANE, MODES, 2 * COLS), jnp.bfloat16),
            pltpu.VMEM((PLANE, MODES, 2 * COLS), jnp.bfloat16),
            pltpu.SemaphoreType.DMA((slots,)),
            pltpu.SemaphoreType.DMA((SIDE,)),
            pltpu.SemaphoreType.DMA((8,)),
            pltpu.SemaphoreType.DMA((14,)),
            pltpu.SemaphoreType.REGULAR,
        ],
        compiler_params=pltpu.CompilerParams(collective_id=0, has_side_effects=True, vmem_limit_bytes=16 * 1024 * 1024),
    )(*(pltpu.with_memory_space_constraint(v, pltpu.HBM) for v in (field.reshape(ROWS * PLANE, COLS), even_vectors, odd_vectors)))
    parts = 2
    rows = MODES // parts
    out = jax.ShapeDtypeStruct((MODES * PLANE, COLS), jnp.float32)
    even_modes, odd_modes = pl.pallas_call(
        unpack,
        grid=(parts,),
        out_shape=(out, out),
        in_specs=[pl.BlockSpec((PLANE, rows, 2 * COLS), lambda i: (0, i, 0))],
        out_specs=[pl.BlockSpec((rows * PLANE, COLS), lambda i: (i, 0))] * 2,
        compiler_params=pltpu.CompilerParams(vmem_limit_bytes=8 * 1024 * 1024),
    )(modes)
    return even_modes.reshape(MODES, PLANE, COLS), odd_modes.reshape(MODES, PLANE, COLS)


def solution(mesh):
    return jax.shard_map(
        local,
        mesh=mesh,
        in_specs=(P("gx", None, "gz"), P("gx", "gz"), P("gx", "gz")),
        out_specs=(P("gx", None, "gz"), P("gx", None, "gz")),
        check_vma=False,
    )
```

```python
import jax
import jax.numpy as jnp
from jax import lax
from jax.experimental import pallas as pl
from jax.experimental.pallas import tpu as pltpu
from jax.sharding import PartitionSpec as P

MESH = pl.DeviceIdType.MESH
SIDE = 4
PLANE = 16
DEEP = 8
GROUP = 4
ROWS = 64
COLS = 128
MODES = 32
CHUNKS = 16
PER = PLANE // CHUNKS
HOPS = 8
FAR_FIRST = (2, 3, 1, 0)


def remote(src, dst, send, recv, target):
    return pltpu.make_async_remote_copy(
        src_ref=src, dst_ref=dst, send_sem=send, recv_sem=recv,
        device_id=target, device_id_type=MESH,
    )


def drain(ref, sem):
    pltpu.make_async_copy(ref, ref, sem).wait()


def kernel(field, even_hbm, odd_hbm, out,
           raw, even, odd, wide, mine, own, far, relay, vecs, acc, sent, got,
           ring_recv, far_recv, recv, send, ready):
    fetches = [
        pltpu.make_async_copy(field, raw, send.at[9]),
        pltpu.make_async_copy(even_hbm, even, send.at[11]),
        pltpu.make_async_copy(odd_hbm, odd, send.at[12]),
    ]
    for fetch in fetches:
        fetch.start()
    gx, gz = lax.axis_index("gx"), lax.axis_index("gz")
    half = gx // PLANE
    q = lax.rem(gx, PLANE)
    qy, qx = q // SIDE, lax.rem(q, SIDE)
    depth, core = gz // 2, lax.rem(gz, 2)
    z = half * DEEP + depth
    step = 2 * core - 1

    def at(place, level):
        return ((level // DEEP) * PLANE + place, lax.rem(level, DEEP) * 2 + core)

    def level(k):
        return lax.rem(z + k * step + 2 * DEEP, 2 * DEEP)

    def offset(i):
        if isinstance(i, int):
            return FAR_FIRST[i]
        return (1 - i // 2) * (2 + i) + (i // 2) * (3 - i)

    def place(t):
        return lax.rem(qy + offset(t // SIDE), SIDE) * SIDE + lax.rem(qx + offset(t % SIDE if isinstance(t, int) else lax.rem(t, SIDE)), SIDE)

    group = depth // GROUP
    ahead, behind = level(1), level(-1)
    across = half * DEEP + lax.rem(depth + GROUP, DEEP)
    mates = [half * DEEP + group * GROUP + lax.rem(depth + k, GROUP) for k in range(1, GROUP)]
    twin = (gx, gz + 1 - 2 * core)
    myrows = pl.ds(pl.multiple_of(q * MODES, MODES), MODES)

    barrier = pltpu.get_barrier_semaphore()

    def hello(target):
        pl.semaphore_signal(barrier, inc=1, device_id=target, device_id_type=MESH)

    hello(at(q, across))
    for m in mates:
        hello(at(q, m))
    hello(at(q, ahead))
    hello(at(q, behind))
    for t in range(PLANE - 1):
        hello(at(place(t), z))
    hello(twin)

    for fetch in fetches:
        fetch.wait()
    wide[...] = raw[...].astype(jnp.float32)
    for t in range(PLANE):
        mine[t] = wide[pl.ds(place(t), ROWS, stride=PLANE), :].astype(jnp.bfloat16)
    own[q] = mine[PLANE - 1]
    vecs[depth, core, myrows, :] = jnp.concatenate([even[...], odd[...]], axis=1)

    pl.semaphore_wait(barrier, PLANE - 1 + 2 + GROUP + 1)

    for m in mates:
        block = vecs.at[depth, core, myrows]
        remote(block, block, send.at[1], recv.at[0], at(q, m)).start()
    for c in range(CHUNKS):
        remote(mine.at[pl.ds(c * PER, PER)], relay.at[c], send.at[0], ring_recv.at[c], at(q, ahead)).start()
    pl.semaphore_signal(ready, inc=1, device_id=at(q, behind), device_id_type=MESH)
    for t in range(PLANE - 1):
        remote(mine.at[t], own.at[q], send.at[2], recv.at[1], at(place(t), z)).start()

    def spread(g, k):
        block = vecs.at[pl.ds(g * GROUP, GROUP), core, myrows]
        for t in range(PLANE - 1):
            remote(block, block, send.at[3 + k], recv.at[2 + k], at(place(t), z)).start()

    def share(g, k):
        drain(vecs.at[pl.ds(0, GROUP), 0, pl.ds(0, (PLANE - 1) * MODES)], recv.at[2 + k])
        block = vecs.at[pl.ds(g * GROUP, GROUP), core]
        remote(block, block, send.at[5 + k], recv.at[4 + k], twin).start()

    def hop(first, last):
        @pl.loop(first * CHUNKS, last * CHUNKS)
        def _(i):
            drain(relay.at[i], ring_recv.at[i])
            remote(relay.at[i], relay.at[i + CHUNKS], send.at[7], ring_recv.at[i + CHUNKS], at(q, ahead)).start()

    hop(0, 1)
    drain(vecs.at[pl.ds(0, GROUP - 1), 0, pl.ds(0, MODES)], recv.at[0])
    block = vecs.at[pl.ds(group * GROUP, GROUP), core, myrows]
    remote(block, block, send.at[8], recv.at[6], at(q, across)).start()
    spread(group, 0)
    hop(1, 3)
    drain(vecs.at[pl.ds(0, GROUP), 0, pl.ds(0, MODES)], recv.at[6])
    spread(1 - group, 1)
    hop(3, 5)
    share(group, 0)
    hop(5, 6)
    share(1 - group, 1)

    pl.semaphore_wait(ready, 1)

    @pl.loop(0, CHUNKS)
    def _(c):
        i = (HOPS - 2) * CHUNKS + c
        drain(relay.at[i], ring_recv.at[i])
        for h in range(PER):
            remote(relay.at[i, h], far.at[q], send.at[13], far_recv.at[qy], at(place(c * PER + h), ahead)).start()

    drain(own.at[pl.ds(0, PLANE - 1)], recv.at[1])
    drain(vecs.at[pl.ds(0, GROUP), 0], recv.at[4])
    drain(vecs.at[pl.ds(0, GROUP), 0], recv.at[5])
    wide_rows = SIDE * ROWS
    r = lax.broadcasted_iota(jnp.int32, (wide_rows, wide_rows), 0)
    s = lax.broadcasted_iota(jnp.int32, (wide_rows, wide_rows), 1)
    plain = (r == s).astype(jnp.float32).astype(jnp.bfloat16)
    turned = (r + s == wide_rows - 1).astype(jnp.float32).astype(jnp.bfloat16)
    zero = jnp.zeros((ROWS, COLS), jnp.bfloat16)

    def pick(first):
        return jnp.where(first, plain, turned)

    is_low = jnp.full((wide_rows, wide_rows), half, jnp.int32) == 0
    for_own = jnp.where(is_low, plain, turned)
    for_far = jnp.where(is_low, turned, plain)
    sign = (1 - 2 * half).astype(jnp.float32)
    for ty in range(SIDE):
        g = lax.rem(qy - offset(ty) + SIDE, SIDE)
        a = own[pl.ds((SIDE - 1 - g) * SIDE, SIDE)].reshape(wide_rows, COLS)
        a = jnp.dot(for_own, a, preferred_element_type=jnp.float32)
        drain(far.at[pl.ds(0, SIDE)], far_recv.at[g])
        b = far[pl.ds(g * SIDE, SIDE)].reshape(wide_rows, COLS)
        b = jnp.dot(for_far, b, preferred_element_type=jnp.float32)
        plus = (a + b).astype(jnp.bfloat16)
        minus = ((a - b) * sign).astype(jnp.bfloat16)
        j = jnp.where(half == 0, SIDE - 1 - g, g)
        left, right = [], []
        for k in range(2):
            for c in range(2):
                left.append(vecs[2 * j + k, c])
                rows = slice((2 * k + c) * ROWS, (2 * k + c + 1) * ROWS)
                right.append(jnp.concatenate([plus[rows], zero], axis=1))
                right.append(jnp.concatenate([zero, minus[rows]], axis=1))
        part = jnp.dot(jnp.concatenate(left, axis=1), jnp.concatenate(right, axis=0), preferred_element_type=jnp.float32)
        if ty == 0:
            acc[...] = part
        elif ty < SIDE - 1:
            acc[...] += part
        else:
            sent[...] = (acc[...] + part).astype(jnp.bfloat16).reshape(PLANE, MODES, 2 * COLS)

    for t in range(PLANE - 1):
        remote(sent.at[place(t)], got.at[q], send.at[10], recv.at[7], at(place(t), z)).start()
    got[q] = sent[q]
    drain(mine, send.at[0])
    drain(vecs.at[pl.ds(0, GROUP - 1), 0, pl.ds(0, MODES)], send.at[1])
    drain(mine.at[pl.ds(0, PLANE - 1)], send.at[2])
    for k in range(2):
        drain(vecs.at[pl.ds(0, GROUP), 0, pl.ds(0, (PLANE - 1) * MODES)], send.at[3 + k])
        drain(vecs.at[pl.ds(0, GROUP), 0], send.at[5 + k])
    drain(relay.at[pl.ds(0, (HOPS - 2) * CHUNKS)], send.at[7])
    drain(vecs.at[pl.ds(0, GROUP), 0, pl.ds(0, MODES)], send.at[8])
    drain(mine, send.at[13])
    drain(got.at[pl.ds(0, PLANE - 1)], recv.at[7])
    out[...] = got[...]

    drain(got.at[pl.ds(0, PLANE - 1)], send.at[10])


def unpack(got, out_even, out_odd):
    rows = got.shape[1]
    for p in range(PLANE):
        block = got[p].astype(jnp.float32)
        out_even[pl.ds(p, rows, stride=PLANE), :] = block[:, :COLS]
        out_odd[pl.ds(p, rows, stride=PLANE), :] = block[:, COLS:]


def local(field, even_vectors, odd_vectors):
    vmem = pl.BlockSpec(memory_space=pltpu.VMEM)
    slots = (HOPS - 1) * CHUNKS
    modes = pl.pallas_call(
        kernel,
        out_shape=jax.ShapeDtypeStruct((PLANE, MODES, 2 * COLS), jnp.bfloat16),
        in_specs=[pl.BlockSpec(memory_space=pltpu.HBM)] * 3,
        out_specs=vmem,
        scratch_shapes=[
            pltpu.VMEM((ROWS * PLANE, COLS), jnp.bfloat16),
            pltpu.VMEM((MODES, ROWS), jnp.bfloat16),
            pltpu.VMEM((MODES, ROWS), jnp.bfloat16),
            pltpu.VMEM((ROWS * PLANE, COLS), jnp.float32),
            pltpu.VMEM((PLANE, ROWS, COLS), jnp.bfloat16),
            pltpu.VMEM((PLANE, ROWS, COLS), jnp.bfloat16),
            pltpu.VMEM((PLANE, ROWS, COLS), jnp.bfloat16),
            pltpu.VMEM((slots, PER, ROWS, COLS), jnp.bfloat16),
            pltpu.VMEM((DEEP, 2, PLANE * MODES, COLS), jnp.bfloat16),
            pltpu.VMEM((PLANE * MODES, 2 * COLS), jnp.float32),
            pltpu.VMEM((PLANE, MODES, 2 * COLS), jnp.bfloat16),
            pltpu.VMEM((PLANE, MODES, 2 * COLS), jnp.bfloat16),
            pltpu.SemaphoreType.DMA((slots,)),
            pltpu.SemaphoreType.DMA((SIDE,)),
            pltpu.SemaphoreType.DMA((8,)),
            pltpu.SemaphoreType.DMA((14,)),
            pltpu.SemaphoreType.REGULAR,
        ],
        compiler_params=pltpu.CompilerParams(collective_id=0, has_side_effects=True, vmem_limit_bytes=16 * 1024 * 1024),
    )(*(pltpu.with_memory_space_constraint(v, pltpu.HBM) for v in (field.reshape(ROWS * PLANE, COLS), even_vectors, odd_vectors)))
    parts = 2
    rows = MODES // parts
    out = jax.ShapeDtypeStruct((MODES * PLANE, COLS), jnp.float32)
    even_modes, odd_modes = pl.pallas_call(
        unpack,
        grid=(parts,),
        out_shape=(out, out),
        in_specs=[pl.BlockSpec((PLANE, rows, 2 * COLS), lambda i: (0, i, 0))],
        out_specs=[pl.BlockSpec((rows * PLANE, COLS), lambda i: (i, 0))] * 2,
        compiler_params=pltpu.CompilerParams(vmem_limit_bytes=8 * 1024 * 1024),
    )(modes)
    return even_modes.reshape(MODES, PLANE, COLS), odd_modes.reshape(MODES, PLANE, COLS)


def solution(mesh):
    return jax.shard_map(
        local,
        mesh=mesh,
        in_specs=(P("gx", None, "gz"), P("gx", "gz"), P("gx", "gz")),
        out_specs=(P("gx", None, "gz"), P("gx", None, "gz")),
        check_vma=False,
    )
```
